32 devices in a mesh: seq: 8 (over z, x), chan: 4 (over y, core).
Axes of the slice: x: 2, y: 2, z: 4, core: 2. Of those that a mesh axis runs over, the one named last changes fastest.
Arguments:
- tokens: bfloat16 [2048, 8192], P('seq', 'chan'), may hold values from -700 to 700
- cotangent: bfloat16 [2048, 8192], P('seq', 'chan'), may hold values from -6 to 6
- filters: bfloat16 [256, 8192], P(None, 'chan'), may hold values from -0.375 to 0.375
- gain: float32 [8192], P('chan'), may hold values from 0.25 to 1.75
Outputs:
- conv_out: bfloat16 [2048, 8192], P('seq', 'chan')
- input_grad: bfloat16 [2048, 8192], P('seq', 'chan')
- filter_grad: float32 [256, 8192], P(None, 'chan')
- gain_grad: float32 [8192], P('chan')
The draws below stay inside these ranges and needn't reach their ends.
All inputs are finite; a program needn't handle non-finite values.
Results may differ from the reference program's by a relative error of at most 0.005.
Values may be sent and summed in bfloat16 or wider, within the bound.
A program may use at most 64 MiB of HBM per device.

```python
import math
import jax
import jax.numpy as jnp
from jax import lax

D = 8192
TOKENS = 2048
FLEN = 256


def draw_tokens(key, part):
    first, second, third = jax.random.split(jax.random.fold_in(key, 11), 3)
    column = jnp.arange(D, dtype=jnp.float32) / D
    col_scale = jnp.exp(math.log(10.0) * column) * jax.random.uniform(second, (D,), jnp.float32, 0.6, 1.4)
    row_scale = jnp.exp(math.log(10.0) * jax.random.uniform(third, (TOKENS, 1), jnp.float32))
    base = jnp.clip(jax.random.normal(first, (TOKENS, D), jnp.float32), -5.0, 5.0)
    return (base * row_scale * col_scale[None, :]).astype(jnp.bfloat16)


def shard_levels(own_key, shape, shards, smallest, top_value):
    factor_of, own = 1.0, jax.random.fold_in(own_key, 6)
    for axis_at, parts in shards:
        steps = jnp.exp(jax.random.uniform(jax.random.fold_in(own, axis_at), (parts,), jnp.float32, smallest / len(shards), top_value / len(shards)))
        factor_of = factor_of * jnp.repeat(steps, shape[axis_at] // parts).reshape([-1 if axis == axis_at else 1 for axis in range(len(shape))])
    return factor_of


def scatter_about(rng, extent, deviation, most, cuts=(), held_as=jnp.bfloat16):
    values = deviation * jax.random.normal(rng, extent, jnp.float32)
    if cuts:
        values = values * shard_levels(rng, extent, cuts, -0.22, 0.18)
    return jnp.clip(values, -most, most).astype(held_as)


def setup_inputs(seed: int = 0) -> dict:
    streams_of = jax.random.split(jax.random.key(seed), 5)
    return {
        "tokens": draw_tokens(jax.random.fold_in(streams_of[4], 71), 0),
        "cotangent": scatter_about(streams_of[1], (TOKENS, D), 1.0, 6.0, ((0, 8), (1, 4))),
        "filters": scatter_about(streams_of[2], (FLEN, D), FLEN ** -0.5, 0.375, ((1, 4),)),
        "gain": jnp.clip(1.0 + 0.15 * jax.random.normal(streams_of[3], (D,), jnp.float32), 0.25, 1.75),
    }


def group_grads(pieces):
    normed, gradient, taps, scaled = pieces
    length = 2 * TOKENS
    spec_in = jnp.fft.rfft(normed, n=length, axis=0)
    spec_taps = jnp.fft.rfft(taps, n=length, axis=0)
    spec_grad = jnp.fft.rfft(gradient, n=length, axis=0)
    conv_full = jnp.fft.irfft(spec_in * spec_taps, n=length, axis=0)[:TOKENS]
    upstream = jnp.fft.irfft(spec_grad * jnp.conj(spec_taps), n=length, axis=0)[:TOKENS]
    taps_grad = jnp.fft.irfft(spec_grad * jnp.conj(spec_in), n=length, axis=0)[:FLEN]
    gain_part = lax.optimization_barrier(jnp.sum(upstream * scaled, axis=0))
    return (conv_full, upstream, taps_grad, gain_part)

def reference(tokens, cotangent, filters, gain):
    values = tokens.astype(jnp.float32)
    factor = lax.rsqrt(lax.optimization_barrier(jnp.mean(values * values, axis=1, keepdims=True)) + 1e-06)
    rounded = (values * factor * gain).astype(jnp.bfloat16)
    rounded = lax.optimization_barrier(rounded)
    normed = rounded.astype(jnp.float32)
    group = math.gcd(D, 512)
    blocks = D // group

    def split_groups(array):
        return array.reshape(array.shape[0], blocks, group).transpose(1, 0, 2)

    def join_groups(array):
        return array.transpose(1, 0, 2).reshape(array.shape[1], D)
    conv_full, upstream, taps_grad, gain_part = lax.map(group_grads, (split_groups(normed), split_groups(cotangent.astype(jnp.float32)), split_groups(filters.astype(jnp.float32)), split_groups(values * factor)))
    norm_factor = 1.0 / math.sqrt(TOKENS)
    conv_out = join_groups(conv_full).astype(jnp.bfloat16)
    input_grad = join_groups(upstream).astype(jnp.bfloat16)
    filter_grad = join_groups(taps_grad) * norm_factor
    gain_grad = gain_part.reshape(D) * norm_factor
    return (conv_out, input_grad, filter_grad, gain_grad)
```

```python
import functools
import math

import jax
import jax.numpy as jnp
import ml_dtypes
import numpy as np
from jax import lax
from jax.experimental import pallas as pl
from jax.experimental.pallas import tpu as pltpu
from jax.sharding import PartitionSpec as P

MESH = pl.DeviceIdType.MESH


def halves(matrix):
    high = matrix.astype(ml_dtypes.bfloat16)
    low = (matrix - high.astype(np.float64)).astype(ml_dtypes.bfloat16)
    return high, low


def transforms(rows):
    odd = 2 * np.arange(rows)[:, None] + 1
    angle = np.pi / (2 * rows) * ((odd * np.arange(rows)[None, :]) % (4 * rows))
    forward = np.concatenate([np.cos(angle), -np.sin(angle)], axis=0)
    return (*halves(forward), *halves(forward.T / rows))


def kernel(
    sizes,
    tok, cot, fil, gain, fh, fl, ih, il,
    conv, igrad, fgrad, ggrad,
    htok, hcot, hfac, ssq, fac, spec_h, spec_a, spec_g, part, rs, ag, gsum,
    tok_s, tok_r, cot_s, cot_r, fac_s, fac_r, ssq_s, ssq_r, rs_s, rs_r, ag_s, ag_r, gs_s, gs_r,
):
    shards, groups, chunks, width, piece, owners, model_width, scale = sizes
    rows = tok.shape[0]
    me, my_chan = lax.axis_index("seq"), lax.axis_index("chan")
    nxt, prv = lax.rem(me + 1, shards), lax.rem(me + shards - 1, shards)
    sign = (1 - 2 * (lax.broadcasted_iota(jnp.int32, (rows, width), 0) & 1)).astype(jnp.float32)

    def cols(k):
        return pl.ds(pl.multiple_of(k * width, width), width)

    def every(count, body):
        lax.fori_loop(0, count, lambda i, c: (body(i), c)[1], 0)

    def others(count, mine, body):
        def step(i):
            @pl.when(i != mine)
            def _():
                body(i)
        every(count, step)

    def remote(src, dst, ssem, rsem, seq, chan):
        return pltpu.make_async_remote_copy(
            src_ref=src, dst_ref=dst, send_sem=ssem, recv_sem=rsem, device_id=(seq, chan), device_id_type=MESH)

    def cot_copy(k):
        return remote(cot.at[:, cols(k)], hcot.at[k], cot_s.at[k], cot_r.at[k], prv, my_chan)

    def tok_copy(k):
        return remote(tok.at[:, cols(k)], htok.at[k], tok_s.at[k], tok_r.at[k], nxt, my_chan)

    def fac_copy():
        return remote(fac, hfac, fac_s, fac_r, nxt, my_chan)

    def ssq_copy(to, at):
        return remote(ssq.at[at], ssq.at[at], ssq_s.at[to], ssq_r.at[at], me, to)

    def owned(o):
        return pl.ds(pl.multiple_of(o * piece, piece), piece)

    def rs_copy(k, to, at):
        return remote(part.at[k, owned(to)], rs.at[k, at], rs_s.at[k, to], rs_r.at[k, at], to, my_chan)

    def ag_copy(k, to, at):
        return remote(ag.at[k, owned(at)], ag.at[k, owned(at)], ag_s.at[k, to], ag_r.at[k, at], to, my_chan)

    def gs_copy(to, at):
        return remote(gsum.at[at], gsum.at[at], gs_s.at[to], gs_r.at[at], to, my_chan)

    def forward(x):
        return (jnp.dot(fh[...], x, preferred_element_type=jnp.float32)
                + jnp.dot(fl[...], x, preferred_element_type=jnp.float32))

    def inverse(real, imag):
        both = jnp.concatenate([real, imag], axis=0)
        high = both.astype(jnp.bfloat16)
        low = (both - high.astype(jnp.float32)).astype(jnp.bfloat16)
        return (jnp.dot(ih[...], high, preferred_element_type=jnp.float32)
                + jnp.dot(ih[...], low, preferred_element_type=jnp.float32)
                + jnp.dot(il[...], high, preferred_element_type=jnp.float32))

    def column(row):
        return jnp.transpose(jnp.broadcast_to(row, (128, rows)))[:, 0:1]

    barrier = pltpu.get_barrier_semaphore()
    others(shards, me, lambda p: pl.semaphore_signal(barrier, inc=1, device_id=(p, my_chan), device_id_type=MESH))
    others(groups, my_chan, lambda p: pl.semaphore_signal(barrier, inc=1, device_id=(me, p), device_id_type=MESH))
    pl.semaphore_wait(barrier, shards + groups - 2)

    @pl.when(me > 0)
    def _():
        every(chunks, lambda k: cot_copy(k).start())

    @pl.when(me < shards - 1)
    def _():
        every(chunks, lambda k: tok_copy(k).start())

    @pl.when(me == 0)
    def _():
        htok[...] = jnp.zeros_like(htok)
        hfac[...] = jnp.zeros_like(hfac)

    @pl.when(me == shards - 1)
    def _():
        hcot[...] = jnp.zeros_like(hcot)

    def squares(k, total):
        v = tok[:, cols(k)].astype(jnp.float32)
        return total + jnp.sum(v * v, axis=1, keepdims=True)

    total = lax.fori_loop(0, chunks, squares, jnp.zeros((rows, 1), jnp.float32))
    ssq[my_chan] = jnp.transpose(jnp.broadcast_to(total, (rows, 128)))[0:8]
    others(groups, my_chan, lambda p: ssq_copy(p, my_chan).start())

    def first(k):
        spec_h[k] = forward(fil[:, cols(k)])
        spec_g[k] = forward(cot[:, cols(k)])

    every(chunks, first)
    others(groups, my_chan, lambda p: ssq_copy(my_chan, p).wait_recv())
    fac[...] = lax.rsqrt(jnp.sum(ssq[...], axis=0) / model_width + 1e-06)

    @pl.when(me < shards - 1)
    def _():
        fac_copy().start()

    own_fac = column(fac[0:1])

    def second(k):
        at = cols(k)
        normed = (tok[:, at].astype(jnp.float32) * own_fac * gain[:, at]).astype(jnp.bfloat16)
        spec_a[k] = forward(normed)

    every(chunks, second)

    def backward(k):
        at = cols(k)

        @pl.when(me < shards - 1)
        def _():
            cot_copy(k).wait_recv()
        later = forward(hcot[k])
        g_r = spec_g[k, :rows] + sign * later[rows:]
        g_i = spec_g[k, rows:] - sign * later[:rows]
        a_r, a_i = spec_a[k, :rows], spec_a[k, rows:]
        terms = inverse(g_r * a_r + g_i * a_i, g_i * a_r - g_r * a_i) * scale
        part[k] = terms.astype(jnp.bfloat16)
        others(owners, me, lambda o: rs_copy(k, o, me).start())
        h_r, h_i = spec_h[k, :rows], spec_h[k, rows:]
        upstream = inverse(g_r * h_r + g_i * h_i, g_i * h_r - g_r * h_i)
        igrad[:, at] = upstream.astype(jnp.bfloat16)
        unit = tok[:, at].astype(jnp.float32) * own_fac
        gsum[me, :, at] = jnp.sum(upstream * unit, axis=0, keepdims=True) * scale

    every(chunks, backward)
    others(shards, me, lambda p: gs_copy(p, me).start())

    @pl.when(me > 0)
    def _():
        fac_copy().wait_recv()
    past_fac = column(hfac[0:1])

    def onward(k):
        at = cols(k)

        @pl.when(me > 0)
        def _():
            tok_copy(k).wait_recv()
        normed = (htok[k].astype(jnp.float32) * past_fac * gain[:, at]).astype(jnp.bfloat16)
        past = forward(normed)
        x_r = spec_a[k, :rows] - sign * past[rows:]
        x_i = spec_a[k, rows:] + sign * past[:rows]
        h_r, h_i = spec_h[k, :rows], spec_h[k, rows:]
        conv[:, at] = inverse(x_r * h_r - x_i * h_i, x_r * h_i + x_i * h_r).astype(jnp.bfloat16)

    def gather(k):
        @pl.when(me < owners)
        def _():
            others(shards, me, lambda p: rs_copy(k, me, p).wait_recv())
            rs[k, me] = part[k, owned(me)]
            summed = lax.fori_loop(
                0, shards, lambda p, acc: acc + rs[k, p].astype(jnp.float32), jnp.zeros((piece, width), jnp.float32))
            ag[k, owned(me)] = summed.astype(jnp.bfloat16)
            others(shards, me, lambda p: ag_copy(k, p, me).start())

    def both(k):
        gather(k)
        onward(k)

    every(chunks, both)
    others(shards, me, lambda p: gs_copy(me, p).wait_recv())
    ggrad[...] = jnp.sum(gsum[...], axis=0)

    def finish(k):
        others(owners, me, lambda o: ag_copy(k, me, o).wait_recv())
        fgrad[:, cols(k)] = ag[k].astype(jnp.float32)

    every(chunks, finish)

    others(groups, my_chan, lambda p: ssq_copy(p, my_chan).wait_send())
    others(shards, me, lambda p: gs_copy(p, me).wait_send())

    @pl.when(me > 0)
    def _():
        every(chunks, lambda k: cot_copy(k).wait_send())

    @pl.when(me < shards - 1)
    def _():
        every(chunks, lambda k: tok_copy(k).wait_send())
        fac_copy().wait_send()

    def drained(k):
        others(owners, me, lambda o: rs_copy(k, o, me).wait_send())

        @pl.when(me < owners)
        def _():
            others(shards, me, lambda p: ag_copy(k, p, me).wait_send())

    every(chunks, drained)


def local(tokens, cotangent, filters, gain):
    rows, channels = tokens.shape
    shards, groups = lax.axis_size("seq"), lax.axis_size("chan")
    width = 512 if channels % 512 == 0 else channels
    chunks = channels // width
    piece = max(16, rows // shards)
    owners = rows // piece
    sizes = (shards, groups, chunks, width, piece, owners, channels * groups, 1.0 / math.sqrt(rows * shards))
    vmem = pl.BlockSpec(memory_space=pltpu.VMEM)
    f32, bf16 = jnp.float32, jnp.bfloat16
    dma = pltpu.SemaphoreType.DMA
    conv, igrad, fgrad, ggrad = pl.pallas_call(
        functools.partial(kernel, sizes),
        out_shape=(
            jax.ShapeDtypeStruct((rows, channels), bf16),
            jax.ShapeDtypeStruct((rows, channels), bf16),
            jax.ShapeDtypeStruct((rows, channels), f32),
            jax.ShapeDtypeStruct((1, channels), f32),
        ),
        in_specs=[vmem] * 8,
        out_specs=(vmem,) * 4,
        scratch_shapes=[
            pltpu.VMEM((chunks, rows, width), bf16),
            pltpu.VMEM((chunks, rows, width), bf16),
            pltpu.VMEM((8, rows), f32),
            pltpu.VMEM((groups, 8, rows), f32),
            pltpu.VMEM((8, rows), f32),
            pltpu.VMEM((chunks, 2 * rows, width), f32),
            pltpu.VMEM((chunks, 2 * rows, width), f32),
            pltpu.VMEM((chunks, 2 * rows, width), f32),
            pltpu.VMEM((chunks, rows, width), bf16),
            pltpu.VMEM((chunks, shards, piece, width), bf16),
            pltpu.VMEM((chunks, rows, width), bf16),
            pltpu.VMEM((shards, 1, channels), f32),
            dma((chunks,)), dma((chunks,)), dma((chunks,)), dma((chunks,)),
            dma, dma,
            dma((groups,)), dma((groups,)),
            dma((chunks, owners)), dma((chunks, shards)),
            dma((chunks, shards)), dma((chunks, owners)),
            dma((shards,)), dma((shards,)),
        ],
        compiler_params=pltpu.CompilerParams(
            collective_id=0, has_side_effects=True, vmem_limit_bytes=56 * 1024 * 1024),
    )(tokens, cotangent, filters, gain[None], *(jnp.asarray(m) for m in transforms(rows)))
    return conv, igrad, fgrad, ggrad[0]


def solution(mesh):
    placed = (P("seq", "chan"), P("seq", "chan"), P(None, "chan"), P("chan"))
    return jax.shard_map(
        local,
        mesh=mesh,
        in_specs=placed,
        out_specs=(P("seq", "chan"), P("seq", "chan"), P(None, "chan"), P("chan")),
        check_vma=False,
    )
```

```python
import functools
import math

import jax
import jax.numpy as jnp
import ml_dtypes
import numpy as np
from jax import lax
from jax.experimental import pallas as pl
from jax.experimental.pallas import tpu as pltpu
from jax.sharding import PartitionSpec as P

MESH = pl.DeviceIdType.MESH


def halves(matrix):
    high = matrix.astype(ml_dtypes.bfloat16)
    low = (matrix - high.astype(np.float64)).astype(ml_dtypes.bfloat16)
    return high, low


def transforms(rows):
    odd = 2 * np.arange(rows)[:, None] + 1
    angle = np.pi / (2 * rows) * ((odd * np.arange(rows)[None, :]) % (4 * rows))
    forward = np.concatenate([np.cos(angle), -np.sin(angle)], axis=0)
    return (*halves(forward), *halves(forward.T / rows))


def kernel(
    sizes,
    tok, cot, fil, gain, fh, fl, ih, il,
    conv, igrad, fgrad, ggrad,
    htok, hcot, hfac, ssq, fac, spec_h, spec_a, spec_g, part, rs, mine, near, ag, gsum,
    tok_s, tok_r, cot_s, cot_r, fac_s, fac_r, ssq_s, ssq_r, near_s, near_r, rs_s, rs_r, ag_s, ag_r, gs_s, gs_r,
):
    shards, groups, chunks, width, piece, owners, model_width, scale = sizes
    rows = tok.shape[0]
    me, my_chan = lax.axis_index("seq"), lax.axis_index("chan")
    pairs, side, spot = shards // 2, lax.rem(me, 2), lax.div(me, 2)
    twin = me + 1 - 2 * side
    nxt, prv = lax.rem(me + 1, shards), lax.rem(me + shards - 1, shards)
    sign = (1 - 2 * (lax.broadcasted_iota(jnp.int32, (rows, width), 0) & 1)).astype(jnp.float32)

    def cols(k):
        return pl.ds(pl.multiple_of(k * width, width), width)

    def every(count, body):
        lax.fori_loop(0, count, lambda i, c: (body(i), c)[1], 0)

    def others(count, mine, body):
        def step(i):
            @pl.when(i != mine)
            def _():
                body(i)
        every(count, step)

    def remote(src, dst, ssem, rsem, seq, chan):
        return pltpu.make_async_remote_copy(
            src_ref=src, dst_ref=dst, send_sem=ssem, recv_sem=rsem, device_id=(seq, chan), device_id_type=MESH)

    def cot_copy(k):
        return remote(cot.at[:, cols(k)], hcot.at[k], cot_s.at[k], cot_r.at[k], prv, my_chan)

    def tok_copy(k):
        return remote(tok.at[:, cols(k)], htok.at[k], tok_s.at[k], tok_r.at[k], nxt, my_chan)

    def fac_copy():
        return remote(fac, hfac, fac_s, fac_r, nxt, my_chan)

    def ssq_copy(to, at):
        return remote(ssq.at[at], ssq.at[at], ssq_s.at[to], ssq_r.at[at], me, to)

    def owned(o):
        return pl.ds(pl.multiple_of(o * piece, piece), piece)

    def near_copy(k):
        return remote(mine.at[k], near.at[k], near_s.at[k], near_r.at[k], twin, my_chan)

    def rs_copy(k, to, at):
        return remote(part.at[k, owned(to)], rs.at[k, at], rs_s.at[k, to], rs_r.at[k, at], 2 * to + side, my_chan)

    def ag_copy(k, to, at):
        block = ag.at[k, owned(at)]
        return remote(block, block, ag_s.at[k, to], ag_r.at[k, at], 2 * to + side, my_chan)

    def gs_copy(to, at):
        return remote(gsum.at[at], gsum.at[at], gs_s.at[to], gs_r.at[at], to, my_chan)

    def forward(x):
        return (jnp.dot(fh[...], x, preferred_element_type=jnp.float32)
                + jnp.dot(fl[...], x, preferred_element_type=jnp.float32))

    def inverse(real, imag):
        both = jnp.concatenate([real, imag], axis=0)
        high = both.astype(jnp.bfloat16)
        low = (both - high.astype(jnp.float32)).astype(jnp.bfloat16)
        return (jnp.dot(ih[...], high, preferred_element_type=jnp.float32)
                + jnp.dot(ih[...], low, preferred_element_type=jnp.float32)
                + jnp.dot(il[...], high, preferred_element_type=jnp.float32))

    def column(row):
        return jnp.transpose(jnp.broadcast_to(row, (128, rows)))[:, 0:1]

    barrier = pltpu.get_barrier_semaphore()
    others(shards, me, lambda p: pl.semaphore_signal(barrier, inc=1, device_id=(p, my_chan), device_id_type=MESH))
    others(groups, my_chan, lambda p: pl.semaphore_signal(barrier, inc=1, device_id=(me, p), device_id_type=MESH))
    pl.semaphore_wait(barrier, shards + groups - 2)

    def send_cot(k):
        @pl.when(me > 0)
        def _():
            cot_copy(k).start()

    def send_tok(k):
        @pl.when(me < shards - 1)
        def _():
            tok_copy(k).start()

    every(chunks, send_cot)

    @pl.when(me == 0)
    def _():
        htok[...] = jnp.zeros_like(htok)
        hfac[...] = jnp.zeros_like(hfac)

    @pl.when(me == shards - 1)
    def _():
        hcot[...] = jnp.zeros_like(hcot)

    def squares(k, total):
        v = tok[:, cols(k)].astype(jnp.float32)
        return total + jnp.sum(v * v, axis=1, keepdims=True)

    total = lax.fori_loop(0, chunks, squares, jnp.zeros((rows, 1), jnp.float32))
    ssq[my_chan] = jnp.transpose(jnp.broadcast_to(total, (rows, 128)))[0:8]
    others(groups, my_chan, lambda p: ssq_copy(p, my_chan).start())

    def first(k):
        spec_h[k] = forward(fil[:, cols(k)])
        spec_g[k] = forward(cot[:, cols(k)])

    first(0)
    others(groups, my_chan, lambda p: ssq_copy(my_chan, p).wait_recv())
    fac[...] = lax.rsqrt(jnp.sum(ssq[...], axis=0) / model_width + 1e-06)

    @pl.when(me < shards - 1)
    def _():
        fac_copy().start()

    own_fac = column(fac[0:1])

    def second(k):
        at = cols(k)
        normed = (tok[:, at].astype(jnp.float32) * own_fac * gain[:, at]).astype(jnp.bfloat16)
        spec_a[k] = forward(normed)

    def backward(k):
        at = cols(k)

        @pl.when(me < shards - 1)
        def _():
            cot_copy(k).wait_recv()
        later = forward(hcot[k])
        g_r = spec_g[k, :rows] + sign * later[rows:]
        g_i = spec_g[k, rows:] - sign * later[:rows]
        a_r, a_i = spec_a[k, :rows], spec_a[k, rows:]
        terms = inverse(g_r * a_r + g_i * a_i, g_i * a_r - g_r * a_i) * scale
        part[k] = terms.astype(jnp.bfloat16)
        others(owners, spot, lambda o: rs_copy(k, o, spot).start())
        h_r, h_i = spec_h[k, :rows], spec_h[k, rows:]
        upstream = inverse(g_r * h_r + g_i * h_i, g_i * h_r - g_r * h_i)
        igrad[:, at] = upstream.astype(jnp.bfloat16)
        unit = tok[:, at].astype(jnp.float32) * own_fac
        gsum[me, :, at] = jnp.sum(upstream * unit, axis=0, keepdims=True) * scale

    def reduce(k):
        @pl.when(spot < owners)
        def _():
            others(pairs, spot, lambda p: rs_copy(k, spot, p).wait_recv())
            rs[k, spot] = part[k, owned(spot)]
            summed = lax.fori_loop(
                0, pairs, lambda p, acc: acc + rs[k, p].astype(jnp.float32), jnp.zeros((piece, width), jnp.float32))
            mine[k] = summed.astype(jnp.bfloat16)
            near_copy(k).start()

    for k in range(chunks):
        if k > 0:
            first(k)
        second(k)
        backward(k)
        send_tok(k)
        if k > 1:
            reduce(k - 2)
    others(shards, me, lambda p: gs_copy(p, me).start())

    @pl.when(me > 0)
    def _():
        fac_copy().wait_recv()
    past_fac = column(hfac[0:1])

    def onward(k):
        at = cols(k)

        @pl.when(me > 0)
        def _():
            tok_copy(k).wait_recv()
        normed = (htok[k].astype(jnp.float32) * past_fac * gain[:, at]).astype(jnp.bfloat16)
        past = forward(normed)
        x_r = spec_a[k, :rows] - sign * past[rows:]
        x_i = spec_a[k, rows:] + sign * past[:rows]
        h_r, h_i = spec_h[k, :rows], spec_h[k, rows:]
        conv[:, at] = inverse(x_r * h_r - x_i * h_i, x_r * h_i + x_i * h_r).astype(jnp.bfloat16)

    def gather(k):
        @pl.when(spot < owners)
        def _():
            near_copy(k).wait_recv()
            summed = mine[k].astype(jnp.float32) + near[k].astype(jnp.float32)
            ag[k, owned(spot)] = summed.astype(jnp.bfloat16)
            others(pairs, spot, lambda p: ag_copy(k, p, spot).start())

    behind = [k - 2 for k in range(2, chunks)]
    for k in range(chunks):
        if k not in behind:
            reduce(k)
        if k > 0:
            gather(k - 1)
        onward(k)
    gather(chunks - 1)
    others(shards, me, lambda p: gs_copy(me, p).wait_recv())
    ggrad[...] = jnp.sum(gsum[...], axis=0)

    def finish(k):
        others(owners, spot, lambda o: ag_copy(k, spot, o).wait_recv())
        fgrad[:, cols(k)] = ag[k]

    every(chunks, finish)

    others(groups, my_chan, lambda p: ssq_copy(p, my_chan).wait_send())
    others(shards, me, lambda p: gs_copy(p, me).wait_send())

    @pl.when(me > 0)
    def _():
        every(chunks, lambda k: cot_copy(k).wait_send())

    @pl.when(me < shards - 1)
    def _():
        every(chunks, lambda k: tok_copy(k).wait_send())
        fac_copy().wait_send()

    def drained(k):
        others(owners, spot, lambda o: rs_copy(k, o, spot).wait_send())

        @pl.when(spot < owners)
        def _():
            near_copy(k).wait_send()
            others(pairs, spot, lambda p: ag_copy(k, p, spot).wait_send())

    every(chunks, drained)


def local(tokens, cotangent, filters, gain):
    rows, channels = tokens.shape
    shards, groups = lax.axis_size("seq"), lax.axis_size("chan")
    width = 512 if channels % 512 == 0 else channels
    chunks = channels // width
    pairs = shards // 2
    piece = max(16, rows // pairs)
    owners = rows // piece
    sizes = (shards, groups, chunks, width, piece, owners, channels * groups, 1.0 / math.sqrt(rows * shards))
    vmem = pl.BlockSpec(memory_space=pltpu.VMEM)
    f32, bf16 = jnp.float32, jnp.bfloat16
    dma = pltpu.SemaphoreType.DMA
    conv, igrad, fgrad, ggrad = pl.pallas_call(
        functools.partial(kernel, sizes),
        out_shape=(
            jax.ShapeDtypeStruct((rows, channels), bf16),
            jax.ShapeDtypeStruct((rows, channels), bf16),
            jax.ShapeDtypeStruct((rows, channels), bf16),
            jax.ShapeDtypeStruct((1, channels), f32),
        ),
        in_specs=[vmem] * 8,
        out_specs=(vmem,) * 4,
        scratch_shapes=[
            pltpu.VMEM((chunks, rows, width), bf16),
            pltpu.VMEM((chunks, rows, width), bf16),
            pltpu.VMEM((8, rows), f32),
            pltpu.VMEM((groups, 8, rows), f32),
            pltpu.VMEM((8, rows), f32),
            pltpu.VMEM((chunks, 2 * rows, width), f32),
            pltpu.VMEM((chunks, 2 * rows, width), f32),
            pltpu.VMEM((chunks, 2 * rows, width), f32),
            pltpu.VMEM((chunks, rows, width), bf16),
            pltpu.VMEM((chunks, pairs, piece, width), bf16),
            pltpu.VMEM((chunks, piece, width), bf16),
            pltpu.VMEM((chunks, piece, width), bf16),
            pltpu.VMEM((chunks, rows, width), bf16),
            pltpu.VMEM((shards, 1, channels), f32),
            dma((chunks,)), dma((chunks,)), dma((chunks,)), dma((chunks,)),
            dma, dma,
            dma((groups,)), dma((groups,)),
            dma((chunks,)), dma((chunks,)),
            dma((chunks, owners)), dma((chunks, pairs)),
            dma((chunks, pairs)), dma((chunks, owners)),
            dma((shards,)), dma((shards,)),
        ],
        compiler_params=pltpu.CompilerParams(
            collective_id=0, has_side_effects=True, vmem_limit_bytes=56 * 1024 * 1024),
    )(tokens, cotangent, filters, gain[None], *(jnp.asarray(m) for m in transforms(rows)))
    return conv, igrad, fgrad.astype(f32), ggrad[0]


def solution(mesh):
    placed = (P("seq", "chan"), P("seq", "chan"), P(None, "chan"), P("chan"))
    return jax.shard_map(
        local,
        mesh=mesh,
        in_specs=placed,
        out_specs=(P("seq", "chan"), P("seq", "chan"), P(None, "chan"), P("chan")),
        check_vma=False,
    )
```

```python
import functools
import math

import jax
import jax.numpy as jnp
import ml_dtypes
import numpy as np
from jax import lax
from jax.experimental import pallas as pl
from jax.experimental.pallas import tpu as pltpu
from jax.sharding import PartitionSpec as P

MESH = pl.DeviceIdType.MESH


def halves(matrix):
    high = matrix.astype(ml_dtypes.bfloat16)
    low = (matrix - high.astype(np.float64)).astype(ml_dtypes.bfloat16)
    return high, low


def transforms(rows):
    odd = 2 * np.arange(rows)[:, None] + 1
    angle = np.pi / (2 * rows) * ((odd * np.arange(rows)[None, :]) % (4 * rows))
    forward = np.concatenate([np.cos(angle), -np.sin(angle)], axis=0)
    return (*halves(forward), *halves(forward.T / rows))


def kernel(
    sizes,
    tok, cot, fil, gain, fh, fl, ih, il,
    conv, igrad, fgrad, ggrad,
    htok, hcot, hfac, ssq, fac, spec_h, spec_a, spec_g, part, rs, mine, near, ag, gsum,
    tok_s, tok_r, cot_s, cot_r, fac_s, fac_r, ssq_s, ssq_r, near_s, near_r, rs_s, rs_r, ag_s, ag_r, gs_s, gs_r,
):
    shards, groups, chunks, width, piece, owners, model_width, scale = sizes
    rows = tok.shape[0]
    me, my_chan = lax.axis_index("seq"), lax.axis_index("chan")
    pairs, side, spot = shards // 2, lax.rem(me, 2), lax.div(me, 2)
    twin = me + 1 - 2 * side
    nxt, prv = lax.rem(me + 1, shards), lax.rem(me + shards - 1, shards)
    sign = (1 - 2 * (lax.broadcasted_iota(jnp.int32, (rows, width), 0) & 1)).astype(jnp.float32)

    def cols(k):
        return pl.ds(pl.multiple_of(k * width, width), width)

    def every(count, body):
        lax.fori_loop(0, count, lambda i, c: (body(i), c)[1], 0)

    def others(count, mine, body):
        def step(i):
            @pl.when(i != mine)
            def _():
                body(i)
        every(count, step)

    def remote(src, dst, ssem, rsem, seq, chan):
        return pltpu.make_async_remote_copy(
            src_ref=src, dst_ref=dst, send_sem=ssem, recv_sem=rsem, device_id=(seq, chan), device_id_type=MESH)

    def cot_copy(k):
        return remote(cot.at[:, cols(k)], hcot.at[k], cot_s.at[k], cot_r.at[k], prv, my_chan)

    def tok_copy(k):
        return remote(tok.at[:, cols(k)], htok.at[k], tok_s.at[k], tok_r.at[k], nxt, my_chan)

    def fac_copy():
        return remote(fac, hfac, fac_s, fac_r, nxt, my_chan)

    def ssq_copy(to, at):
        return remote(ssq.at[at], ssq.at[at], ssq_s.at[to], ssq_r.at[at], me, to)

    def owned(o):
        return pl.ds(pl.multiple_of(o * piece, piece), piece)

    def near_copy(k):
        return remote(mine.at[k], near.at[k], near_s.at[k], near_r.at[k], twin, my_chan)

    def rs_copy(k, to, at):
        return remote(part.at[k, owned(to)], rs.at[k, at], rs_s.at[k, to], rs_r.at[k, at], 2 * to + side, my_chan)

    def ag_copy(k, to, at):
        block = ag.at[k, owned(at)]
        return remote(block, block, ag_s.at[k, to], ag_r.at[k, at], 2 * to + side, my_chan)

    def gs_copy(to, at):
        return remote(gsum.at[at], gsum.at[at], gs_s.at[to], gs_r.at[at], to, my_chan)

    def forward(x):
        return (jnp.dot(fh[...], x, preferred_element_type=jnp.float32)
                + jnp.dot(fl[...], x, preferred_element_type=jnp.float32))

    def inverse(real, imag):
        both = jnp.concatenate([real, imag], axis=0)
        high = both.astype(jnp.bfloat16)
        low = (both - high.astype(jnp.float32)).astype(jnp.bfloat16)
        return (jnp.dot(ih[...], high, preferred_element_type=jnp.float32)
                + jnp.dot(ih[...], low, preferred_element_type=jnp.float32)
                + jnp.dot(il[...], high, preferred_element_type=jnp.float32))

    def column(row):
        return jnp.transpose(jnp.broadcast_to(row, (128, rows)))[:, 0:1]

    barrier = pltpu.get_barrier_semaphore()
    others(shards, me, lambda p: pl.semaphore_signal(barrier, inc=1, device_id=(p, my_chan), device_id_type=MESH))
    others(groups, my_chan, lambda p: pl.semaphore_signal(barrier, inc=1, device_id=(me, p), device_id_type=MESH))
    pl.semaphore_wait(barrier, shards + groups - 2)

    def send_cot(k):
        @pl.when(me > 0)
        def _():
            cot_copy(k).start()

    def send_tok(k):
        @pl.when(me < shards - 1)
        def _():
            tok_copy(k).start()

    every(chunks, send_cot)

    @pl.when(me == 0)
    def _():
        htok[...] = jnp.zeros_like(htok)
        hfac[...] = jnp.zeros_like(hfac)

    @pl.when(me == shards - 1)
    def _():
        hcot[...] = jnp.zeros_like(hcot)

    def squares(k, total):
        v = tok[:, cols(k)].astype(jnp.float32)
        return total + jnp.sum(v * v, axis=1, keepdims=True)

    total = lax.fori_loop(0, chunks, squares, jnp.zeros((rows, 1), jnp.float32))
    ssq[my_chan] = jnp.transpose(jnp.broadcast_to(total, (rows, 128)))[0:8]
    others(groups, my_chan, lambda p: ssq_copy(p, my_chan).start())

    def first(k):
        spec_h[k] = forward(fil[:, cols(k)])
        spec_g[k] = forward(cot[:, cols(k)])

    first(0)
    others(groups, my_chan, lambda p: ssq_copy(my_chan, p).wait_recv())
    fac[...] = lax.rsqrt(jnp.sum(ssq[...], axis=0) / model_width + 1e-06)

    @pl.when(me < shards - 1)
    def _():
        fac_copy().start()

    own_fac = column(fac[0:1])

    def second(k):
        at = cols(k)
        normed = (tok[:, at].astype(jnp.float32) * own_fac * gain[:, at]).astype(jnp.bfloat16)
        spec_a[k] = forward(normed)

    def backward(k):
        at = cols(k)

        @pl.when(me < shards - 1)
        def _():
            cot_copy(k).wait_recv()
        later = forward(hcot[k])
        g_r = spec_g[k, :rows] + sign * later[rows:]
        g_i = spec_g[k, rows:] - sign * later[:rows]
        a_r, a_i = spec_a[k, :rows], spec_a[k, rows:]
        terms = inverse(g_r * a_r + g_i * a_i, g_i * a_r - g_r * a_i) * scale
        part[k] = terms.astype(jnp.bfloat16)
        others(owners, spot, lambda o: rs_copy(k, o, spot).start())
        h_r, h_i = spec_h[k, :rows], spec_h[k, rows:]
        upstream = inverse(g_r * h_r + g_i * h_i, g_i * h_r - g_r * h_i)
        igrad[:, at] = upstream.astype(jnp.bfloat16)
        unit = tok[:, at].astype(jnp.float32) * own_fac
        gsum[me, :, at] = jnp.sum(upstream * unit, axis=0, keepdims=True) * scale

    def reduce(k):
        @pl.when(spot < owners)
        def _():
            others(pairs, spot, lambda p: rs_copy(k, spot, p).wait_recv())
            rs[k, spot] = part[k, owned(spot)]
            summed = lax.fori_loop(
                0, pairs, lambda p, acc: acc + rs[k, p].astype(jnp.float32), jnp.zeros((piece, width), jnp.float32))
            mine[k] = summed.astype(jnp.bfloat16)
            near_copy(k).start()

    for k in range(chunks):
        if k > 0:
            first(k)
        second(k)
        backward(k)
        send_tok(k)
        if k > 1:
            reduce(k - 2)
    others(shards, me, lambda p: gs_copy(p, me).start())

    @pl.when(me > 0)
    def _():
        fac_copy().wait_recv()
    past_fac = column(hfac[0:1])

    def onward(k):
        at = cols(k)

        @pl.when(me > 0)
        def _():
            tok_copy(k).wait_recv()
        normed = (htok[k].astype(jnp.float32) * past_fac * gain[:, at]).astype(jnp.bfloat16)
        past = forward(normed)
        x_r = spec_a[k, :rows] - sign * past[rows:]
        x_i = spec_a[k, rows:] + sign * past[:rows]
        h_r, h_i = spec_h[k, :rows], spec_h[k, rows:]
        conv[:, at] = inverse(x_r * h_r - x_i * h_i, x_r * h_i + x_i * h_r).astype(jnp.bfloat16)

    def gather(k):
        @pl.when(spot < owners)
        def _():
            near_copy(k).wait_recv()
            summed = mine[k].astype(jnp.float32) + near[k].astype(jnp.float32)
            ag[k, owned(spot)] = summed.astype(jnp.bfloat16)
            others(pairs, spot, lambda p: ag_copy(k, p, spot).start())

    behind = [k - 2 for k in range(2, chunks)]
    for k in range(chunks):
        if k not in behind:
            reduce(k)
        if k > 0:
            gather(k - 1)
        onward(k)
    gather(chunks - 1)
    others(shards, me, lambda p: gs_copy(me, p).wait_recv())
    ggrad[...] = jnp.sum(gsum[...], axis=0)

    def finish(k):
        others(owners, spot, lambda o: ag_copy(k, spot, o).wait_recv())
        fgrad[:, cols(k)] = ag[k]

    every(chunks, finish)

    others(groups, my_chan, lambda p: ssq_copy(p, my_chan).wait_send())
    others(shards, me, lambda p: gs_copy(p, me).wait_send())

    @pl.when(me > 0)
    def _():
        every(chunks, lambda k: cot_copy(k).wait_send())

    @pl.when(me < shards - 1)
    def _():
        every(chunks, lambda k: tok_copy(k).wait_send())
        fac_copy().wait_send()

    def drained(k):
        others(owners, spot, lambda o: rs_copy(k, o, spot).wait_send())

        @pl.when(spot < owners)
        def _():
            near_copy(k).wait_send()
            others(pairs, spot, lambda p: ag_copy(k, p, spot).wait_send())

    every(chunks, drained)


def local(tokens, cotangent, filters, gain):
    rows, channels = tokens.shape
    shards, groups = lax.axis_size("seq"), lax.axis_size("chan")
    width = 256 if channels % 256 == 0 else channels
    chunks = channels // width
    pairs = shards // 2
    piece = max(16, rows // pairs)
    owners = rows // piece
    sizes = (shards, groups, chunks, width, piece, owners, channels * groups, 1.0 / math.sqrt(rows * shards))
    vmem = pl.BlockSpec(memory_space=pltpu.VMEM)
    f32, bf16 = jnp.float32, jnp.bfloat16
    dma = pltpu.SemaphoreType.DMA
    conv, igrad, fgrad, ggrad = pl.pallas_call(
        functools.partial(kernel, sizes),
        out_shape=(
            jax.ShapeDtypeStruct((rows, channels), bf16),
            jax.ShapeDtypeStruct((rows, channels), bf16),
            jax.ShapeDtypeStruct((rows, channels), bf16),
            jax.ShapeDtypeStruct((1, channels), f32),
        ),
        in_specs=[vmem] * 8,
        out_specs=(vmem,) * 4,
        scratch_shapes=[
            pltpu.VMEM((chunks, rows, width), bf16),
            pltpu.VMEM((chunks, rows, width), bf16),
            pltpu.VMEM((8, rows), f32),
            pltpu.VMEM((groups, 8, rows), f32),
            pltpu.VMEM((8, rows), f32),
            pltpu.VMEM((chunks, 2 * rows, width), f32),
            pltpu.VMEM((chunks, 2 * rows, width), f32),
            pltpu.VMEM((chunks, 2 * rows, width), f32),
            pltpu.VMEM((chunks, rows, width), bf16),
            pltpu.VMEM((chunks, pairs, piece, width), bf16),
            pltpu.VMEM((chunks, piece, width), bf16),
            pltpu.VMEM((chunks, piece, width), bf16),
            pltpu.VMEM((chunks, rows, width), bf16),
            pltpu.VMEM((shards, 1, channels), f32),
            dma((chunks,)), dma((chunks,)), dma((chunks,)), dma((chunks,)),
            dma, dma,
            dma((groups,)), dma((groups,)),
            dma((chunks,)), dma((chunks,)),
            dma((chunks, owners)), dma((chunks, pairs)),
            dma((chunks, pairs)), dma((chunks, owners)),
            dma((shards,)), dma((shards,)),
        ],
        compiler_params=pltpu.CompilerParams(
            collective_id=0, has_side_effects=True, vmem_limit_bytes=56 * 1024 * 1024),
    )(tokens, cotangent, filters, gain[None], *(jnp.asarray(m) for m in transforms(rows)))
    return conv, igrad, fgrad.astype(f32), ggrad[0]


def solution(mesh):
    placed = (P("seq", "chan"), P("seq", "chan"), P(None, "chan"), P("chan"))
    return jax.shard_map(
        local,
        mesh=mesh,
        in_specs=placed,
        out_specs=(P("seq", "chan"), P("seq", "chan"), P(None, "chan"), P("chan")),
        check_vma=False,
    )
```
